512 devices in a mesh: dp: 32 (over y_hi, x, core), section: 2 (over y_lo), tensor: 8 (over z).
Axes of the slice: x: 4, y: 8 (y_hi: 4, y_lo: 2; y = y_hi * 2 + y_lo), z: 8, core: 2. Of those that a mesh axis runs over, the one named last changes fastest.
Arguments:
- own_rows: bfloat16 [2, 8192, 8192], P('section', 'dp', 'tensor'), may hold values from -6 to 6
- out_rows: bfloat16 [2, 8192, 28672], P('section', 'dp', 'tensor'), may hold values from -6 to 6
- val_own: bfloat16 [2, 1024, 8192], P('section', 'dp', 'tensor'), may hold values from -0.01171875 to 0.01171875
- val_out: bfloat16 [2, 1024, 28672], P('section', 'dp', 'tensor'), may hold values from -0.005859375 to 0.005859375
Outputs:
- token_scores: float32 [8192], P(('dp', 'tensor'))
- seq_scores: float32 [32], P('dp')
The draws below stay inside these ranges and needn't reach their ends.
All inputs are finite; a program needn't handle non-finite values.
Results may differ from the reference program's by a relative error of at most 0.0003.
Values may be sent and summed in bfloat16 or wider, within the bound.
A program may use at most 64 MiB of HBM per device.

```python
import jax
import jax.numpy as jnp

D = 8192
FF = 28672
LEN = 256
VTOK = 1024
TOKENS = 8192


def block_levels(own_key, dims, split, least, top_value):
    loudness, own = 1.0, jax.random.fold_in(own_key, 6)
    for dim, parts in split:
        draws = jnp.exp(jax.random.uniform(jax.random.fold_in(own, dim), (parts,), jnp.float32, least / len(split), top_value / len(split)))
        loudness = loudness * jnp.repeat(draws, dims[dim] // parts).reshape([-1 if axis == dim else 1 for axis in range(len(dims))])
    return loudness


def normal_values(stream_key, extent, width, bound, cuts=(), kind=jnp.bfloat16):
    drawn = width * jax.random.normal(stream_key, extent, jnp.float32)
    if cuts:
        drawn = drawn * block_levels(stream_key, extent, cuts, -0.22, 0.18)
    return jnp.clip(drawn, -bound, bound).astype(kind)


def setup_inputs(seed: int = 0) -> dict:
    arg_keys = jax.random.split(jax.random.key(seed), 5)
    own_rows = normal_values(arg_keys[0], (2, TOKENS, D), 1.0, 6.0, ((0, 2), (1, 32), (2, 8)))
    out_rows = normal_values(arg_keys[1], (2, TOKENS, FF), 1.0, 6.0, ((0, 2), (1, 32), (2, 8)))
    val_own = normal_values(arg_keys[2], (2, VTOK, D), (D * 32) ** -0.5, 0.01171875, ((0, 2), (1, 32), (2, 8)))
    val_out = normal_values(arg_keys[3], (2, VTOK, FF), (FF * 32) ** -0.5, 0.005859375, ((0, 2), (1, 32), (2, 8)))
    return dict(own_rows=own_rows, out_rows=out_rows, val_own=val_own, val_out=val_out)


def reference(own_rows, out_rows, val_own, val_out):
    token_total = jnp.zeros((own_rows.shape[1],), jnp.float32)
    for which_layer in range(2):
        partner = 1 - which_layer
        input_gram = jnp.dot(own_rows[which_layer], val_own[which_layer].T, preferred_element_type=jnp.float32)
        output_gram = jnp.dot(out_rows[partner], val_out[partner].T, preferred_element_type=jnp.float32)
        token_total = token_total + jnp.sum(input_gram * output_gram, axis=1)
    seq_scores = jnp.sum(token_total.reshape(-1, LEN), axis=1)
    return token_total, seq_scores
```

```python
import jax
import jax.numpy as jnp
from jax import lax
from jax.sharding import PartitionSpec as P

LEN = 256


def swapped(x, axis, bit):
    return lax.ppermute(x, axis, [(i, i ^ 1 << bit) for i in range(lax.axis_size(axis))])


def in_one_piece(arrays, axis, dim, along):
    both = jnp.concatenate(arrays, axis=along)
    filled, at, outs = (lax.all_gather(both, axis, axis=dim, tiled=True), 0, [])
    for a in arrays:
        outs.append(lax.slice_in_dim(filled, at, at + a.shape[along], axis=along))
        at += a.shape[along]
    return tuple(outs)


def sent_together(arrays, axis, dim, along):
    ends, at = ([], 0)
    for a in arrays[:-1]:
        at += a.shape[along]
        ends.append(at)
    both = jnp.concatenate(arrays, axis=along)
    return tuple(
        jnp.split(lax.psum_scatter(both, axis, scatter_dimension=dim, tiled=True), ends, axis=along)
    )


def over_pieces(x, axis):
    return lax.all_gather(x, axis).sum(0)


def from_everyone(x, axis):
    peers = lax.axis_size(axis)
    return lax.all_to_all(jnp.broadcast_to(x[None], (peers, *x.shape)), axis, 0, 0, tiled=True)


def taken_together(x, axis):
    everything = from_everyone(x, axis)
    return jnp.sum(everything, axis=0)


def row_gram(left_rows, right_rows):
    return lax.dot_general(
        left_rows, right_rows, (((1,), (1,)), ((), ())), preferred_element_type=jnp.float32
    )


def body(own_rows, out_rows, val_own, val_out):
    layer_input = own_rows[0]
    local_output = out_rows[0]
    val_input = val_own[0]
    val_output = val_out[0]
    token_count = layer_input.shape[0]
    pieces = in_one_piece((val_input, val_output), "dp", 0, 1)
    input_block = row_gram(layer_input, pieces[0])
    output_block = row_gram(local_output, pieces[1])
    input_gram = input_block
    output_gram = output_block
    share_rows = token_count // lax.axis_size("tensor")
    input_gram, output_gram = sent_together((input_gram, output_gram), "tensor", 0, 1)
    output_gram = swapped(output_gram, "section", 0)
    layer_scores = jnp.sum(input_gram * output_gram, axis=1)
    token_scores = over_pieces(layer_scores, "section")
    row_index = lax.iota(jnp.int32, share_rows) + lax.axis_index("tensor") * share_rows
    member_mask = (row_index // LEN)[:, None] == lax.iota(jnp.int32, token_count // LEN)[None, :]
    seq_part = jnp.sum(jnp.where(member_mask, token_scores[:, None], jnp.float32(0.0)), axis=0)
    seq_scores = jnp.sum(lax.all_gather(seq_part, "tensor"), axis=0)
    return (token_scores, seq_scores)


def solution(mesh):
    in_specs = (
        P("section", "dp", "tensor"),
        P("section", "dp", "tensor"),
        P("section", "dp", "tensor"),
        P("section", "dp", "tensor"),
    )
    out_specs = (P(("dp", "tensor")), P("dp"))
    return jax.shard_map(body, mesh=mesh, in_specs=in_specs, out_specs=out_specs, check_vma=False)
```

```python
import jax
import jax.numpy as jnp
from jax import lax
from jax.experimental import pallas as pl
from jax.experimental.pallas import tpu as pltpu
from jax.sharding import PartitionSpec as P

NX = 4
NY = 4
NZ = 8
MESH = pl.DeviceIdType.MESH


class Plan:
    def __init__(self, send_sem, recv_sem):
        self.send_sem, self.recv_sem, self.copies = send_sem, recv_sem, {}

    def send(self, name, src, dst, device):
        n = len(self.copies)
        assert n < COPIES
        copy = pltpu.make_async_remote_copy(
            src_ref=src,
            dst_ref=dst,
            send_sem=self.send_sem.at[n],
            recv_sem=self.recv_sem.at[n],
            device_id=device,
            device_id_type=MESH,
        )
        copy.start()
        self.copies[name] = copy

    def arrived(self, name, dst=None):
        if dst is None:
            self.copies[name].wait_recv()
            return
        n = list(self.copies).index(name)
        pltpu.make_async_remote_copy(
            src_ref=dst,
            dst_ref=dst,
            send_sem=self.send_sem.at[n],
            recv_sem=self.recv_sem.at[n],
            device_id={"tensor": lax.axis_index("tensor")},
            device_id_type=MESH,
        ).wait_recv()

    def drain(self):
        for copy in self.copies.values():
            copy.wait_send()


def kernel(
    own_ref, out_ref, vown_ref, vout_ref,
    tokens_ref, seq_ref,
    tok_a, tok_b, val_a, val_b, part, hop, kept, cross, got, tile, tiles, sums,
    local_sem, send_sem, recv_sem,
):
    d, sec, z = lax.axis_index("dp"), lax.axis_index("section"), lax.axis_index("tensor")
    core, x, y = d % 2, (d // 2) % NX, d // (2 * NX)
    rows, share = own_ref.shape[0], vown_ref.shape[0]
    half, block = share // 2, rows // NZ

    def at(yy, xx, cc):
        return {"dp": (yy * NX + xx) * 2 + cc}

    east, west = at(y, (x + 1) % NX, core), at(y, (x + NX - 1) % NX, core)
    north, south = at((y + 1) % NY, x, core), at((y + NY - 1) % NY, x, core)
    sibling = at(y, x, 1 - core)
    partner = {"section": 1 - sec}
    diagonal = {"dp": sibling["dp"], "section": 1 - sec}
    up, down = {"tensor": (z + 1) % NZ}, {"tensor": (z + NZ - 1) % NZ}

    barrier = pltpu.get_barrier_semaphore()
    greeted = (east, west, north, south, sibling, partner, diagonal, up, down)
    for device in greeted:
        pl.semaphore_signal(barrier, inc=1, device_id=device, device_id_type=MESH)

    local = [
        pltpu.make_async_copy(vout_ref, val_b.at[0, pl.ds(0, share)], local_sem.at[0]),
        pltpu.make_async_copy(vown_ref, val_a.at[0, pl.ds(0, share)], local_sem.at[1]),
        pltpu.make_async_copy(out_ref, tok_b.at[pl.ds(0, rows)], local_sem.at[2]),
        pltpu.make_async_copy(own_ref, tok_a.at[pl.ds(0, rows)], local_sem.at[3]),
    ]
    for copy in local:
        copy.start()
    pl.semaphore_wait(barrier, len(greeted))

    plan = Plan(send_sem, recv_sem)

    def slot(kind, dy, dx, h=None):
        ref = val_a if kind == "a" else val_b
        first, count = (dx * share, share) if h is None else (dx * share + h * half, half)
        return ref.at[dy, pl.ds(first, count)]

    def go(kind, dy, dx, h, to, first=False):
        device, sy, sx = {"n": (north, -1, 0), "s": (south, 1, 0), "e": (east, 0, -1), "w": (west, 0, 1)}[to]
        ty, tx = (dy + sy) % NY, (dx + sx) % NX
        src = slot(kind, dy, dx, h)
        if first:
            ref = vown_ref if kind == "a" else vout_ref
            src = ref if h is None else ref.at[pl.ds(h * half, half)]
        plan.send((kind, ty, tx, h), src, slot(kind, ty, tx, h), device)

    def has(kind, dy, dx, h=None):
        plan.arrived((kind, dy, dx, h))

    def multiply(g):
        for c in range(2):
            span = pl.ds(c * rows, rows)
            for k, (tok, val) in enumerate(((tok_a, val_a), (tok_b, val_b))):
                gram = lax.dot_general(
                    tok[span, :], val[g], (((1,), (1,)), ((), ())), preferred_element_type=jnp.float32
                )
                part[g, k, :, pl.ds(c * block, block), :] = gram.reshape(NZ, block, NX * share)

    arcs = ((0, -1, 4, 0), (0, 1, 3, 4), (1, 1, 4, 7), (1, -1, 3, 11))

    def ring(g, t):
        for k, sign, steps, base in arcs:
            if t >= steps:
                continue
            owner = (z + NZ + sign * (steps - t)) % NZ
            src = part.at[g, k, owner]
            if t:
                plan.arrived(("ring", g, base + t - 1))
                src = hop.at[g, base + t - 1]
                src[...] = src[...] + part[g, k, owner]
            plan.send(("ring", g, base + t), src, hop.at[g, base + t], up if sign > 0 else down)

    def reduced(g, k):
        total = part[g, k, z]
        for kk, _, steps, base in arcs:
            if kk == k:
                plan.arrived(("ring", g, base + steps - 1))
                total = total + hop[g, base + steps - 1]
        return total

    def exchange(g):
        cross[g] = reduced(g, 1)
        plan.send(("cross", g), cross.at[g], got.at[g], partner)
        kept[g] = reduced(g, 0)

    def product(g):
        plan.arrived(("cross", g))
        return kept[g] * got[g]

    for h in range(2):
        go("b", 0, 0, h, "n", True)
        go("b", 0, 0, 1 - h, "s", True)
    for to in "ew":
        go("a", 0, 0, None, to, True)
    for h in range(2):
        go("b", 0, 0, h, "e", True)
        go("b", 0, 0, 1 - h, "w", True)
    plan.send(("tok", 1), out_ref, tok_b.at[pl.ds(rows, rows)], sibling)
    plan.send(("tok", 0), own_ref, tok_a.at[pl.ds(rows, rows)], sibling)
    for to in "ns":
        go("a", 0, 0, None, to, True)

    def half_on(kind, axis):
        if axis == "x":
            return lambda dy, h: go(kind, dy, NX - 1, 0, "e") if h == 0 else go(kind, dy, 1, 1, "w")
        return lambda dx, h: go(kind, NY - 1, dx, 0, "n") if h == 0 else go(kind, 1, dx, 1, "s")

    ax, bx, ay, by = half_on("a", "x"), half_on("b", "x"), half_on("a", "y"), half_on("b", "y")

    def b_row(dy, h):
        go("b", dy, 0, h, "e")
        go("b", dy, 0, h, "w")

    has("a", 0, 3)
    ax(0, 0)
    has("a", 0, 1)
    ax(0, 1)
    for dx in (3, 1):
        go("a", 0, dx, None, "n")
        go("a", 0, dx, None, "s")
    has("b", 0, 3, 0)
    bx(0, 0)
    has("b", 0, 1, 1)
    bx(0, 1)
    has("b", 3, 0, 0)
    by(0, 0)
    b_row(3, 0)
    has("b", 1, 0, 1)
    by(0, 1)
    b_row(1, 1)
    has("a", 0, 2, 0)
    has("a", 0, 2, 1)
    for to in "ns":
        go("a", 0, 2, None, to)
    has("b", 3, 0, 1)
    b_row(3, 1)
    has("b", 1, 0, 0)
    b_row(1, 0)

    for h in (0, 1):
        has("b", 0, 3 if h else 1, h)
    has("b", 0, 2, 0)
    has("b", 0, 2, 1)
    for copy in local:
        copy.wait()
    plan.arrived(("tok", 1))
    plan.arrived(("tok", 0))
    multiply(0)
    ring(0, 0)

    has("a", 3, 0)
    ay(0, 0)
    has("a", 1, 0)
    ay(0, 1)
    has("b", 3, 3, 0)
    bx(3, 0)
    has("b", 3, 1, 0)
    has("b", 1, 1, 1)
    bx(1, 1)
    has("b", 1, 3, 1)
    ring(0, 1)
    for dx in (3, 1):
        has("a", 3, dx)
        ay(dx, 0)
        has("a", 1, dx)
        ay(dx, 1)
    has("b", 3, 1, 1)
    bx(3, 1)
    has("b", 3, 3, 1)
    has("b", 1, 3, 0)
    bx(1, 0)
    has("b", 1, 1, 0)
    ring(0, 2)
    has("b", 2, 0, 0)
    b_row(2, 0)
    has("b", 2, 0, 1)
    b_row(2, 1)
    has("a", 3, 2)
    ay(2, 0)
    has("a", 1, 2)
    ay(2, 1)
    ring(0, 3)
    for dy in (3, 1):
        has("b", dy, 2, 0)
        has("b", dy, 2, 1)
        multiply(dy)
        ring(dy, 0)
    exchange(0)
    has("b", 2, 3, 0)
    bx(2, 0)
    has("b", 2, 1, 1)
    bx(2, 1)
    ring(3, 1)
    ring(1, 1)
    for h in (0, 1):
        has("b", 2, 3 if h else 1, h)
    ring(3, 2)
    ring(1, 2)
    for dx in (0, 3, 1, 2):
        has("a", 2, dx, 0)
        has("a", 2, dx, 1)
    ring(3, 3)
    ring(1, 3)
    has("b", 2, 2, 0)
    has("b", 2, 2, 1)
    multiply(2)
    ring(2, 0)
    exchange(3)
    exchange(1)
    ring(2, 1)
    total = product(0)
    ring(2, 2)
    total = total + product(3)
    ring(2, 3)
    total = total + product(1)
    exchange(2)
    total = total + product(2)

    scores = jnp.sum(total.T, axis=0, keepdims=True)
    tile[...] = jnp.zeros_like(tile)
    tile[0:1, 0:block] = scores[:, 0:block]
    tile[1:2, 0:block] = scores[:, block:]
    plan.send("partner", tile, tiles.at[0], partner)
    plan.send("sibling", tile, tiles.at[1], sibling)
    plan.send("diagonal", tile, tiles.at[2], diagonal)
    plan.arrived("partner")
    mine = tile[0:1, :] + tiles[0, 0:1, :]
    plan.arrived("sibling")
    plan.arrived("diagonal")
    mine = mine + (tiles[1, 1:2, :] + tiles[2, 1:2, :])
    tokens_ref[...] = mine[:, 0:block]

    sums[z] = jnp.broadcast_to(mine, (8, mine.shape[1]))
    for r in range(1, NZ):
        plan.send(("sum", r), sums.at[z], sums.at[z], {"tensor": (z + r) % NZ})
    for r in range(1, NZ):
        came = (z + NZ - r) % NZ
        plan.arrived(("sum", r), sums.at[came])
    every = sums[0]
    for r in range(1, NZ):
        every = every + sums[r]
    seq_ref[...] = jnp.sum(every[0:1, :], axis=1, keepdims=True)
    plan.drain()


COPIES = 4 + 2 + 60 + 60 + 4 * 15 + 3 + 7


def body(own_rows, out_rows, val_own, val_out):
    rows, wide_a = own_rows.shape[1:]
    share, wide_b = val_out.shape[1:]
    block, group = rows // NZ, NX * share
    f32, bf16 = jnp.float32, jnp.bfloat16
    hbm = pl.BlockSpec(memory_space=pl.ANY)
    vmem = pl.BlockSpec(memory_space=pltpu.VMEM)
    tokens, seq = pl.pallas_call(
        kernel,
        out_shape=(jax.ShapeDtypeStruct((1, block), f32), jax.ShapeDtypeStruct((1, 1), f32)),
        in_specs=[hbm] * 4,
        out_specs=(vmem, vmem),
        scratch_shapes=[
            pltpu.VMEM((2 * rows, wide_a), bf16),
            pltpu.VMEM((2 * rows, wide_b), bf16),
            pltpu.VMEM((NY, group, wide_a), bf16),
            pltpu.VMEM((NY, group, wide_b), bf16),
            pltpu.VMEM((NY, 2, NZ, 2 * block, group), f32),
            pltpu.VMEM((NY, 14, 2 * block, group), f32),
            pltpu.VMEM((NY, 2 * block, group), f32),
            pltpu.VMEM((NY, 2 * block, group), f32),
            pltpu.VMEM((NY, 2 * block, group), f32),
            pltpu.VMEM((8, 128), f32),
            pltpu.VMEM((3, 8, 128), f32),
            pltpu.VMEM((NZ, 8, 128), f32),
            pltpu.SemaphoreType.DMA((4,)),
            pltpu.SemaphoreType.DMA((COPIES,)),
            pltpu.SemaphoreType.DMA((COPIES,)),
        ],
        compiler_params=pltpu.CompilerParams(
            collective_id=0, has_side_effects=True, vmem_limit_bytes=40 * 1024 * 1024
        ),
    )(own_rows[0], out_rows[0], val_own[0], val_out[0])
    return tokens.reshape(block), seq.reshape(1)


def solution(mesh):
    spec = P("section", "dp", "tensor")
    return jax.shard_map(
        body,
        mesh=mesh,
        in_specs=(spec,) * 4,
        out_specs=(P(("dp", "tensor")), P("dp")),
        check_vma=False,
    )
```

```python
import jax
import jax.numpy as jnp
from jax import lax
from jax.experimental import pallas as pl
from jax.experimental.pallas import tpu as pltpu
from jax.sharding import PartitionSpec as P

NX = 4
NY = 4
NZ = 8
MESH = pl.DeviceIdType.MESH


ARCS = (((-1, 4, 0), (1, 3, 4)), ((1, 4, 7), (-1, 3, 11)))
HOLDS = {("a", "x"): 0.7, ("a", "y"): 1.41, ("b", "x"): 2.47, ("b", "y"): 4.93}
SUM_HOLDS = 0.7
LATENCY = {"x": 2.0, "y": 3.0, "z": 1.8, "c": 1.8}
SLACK = {0: 4.0, 3: 0.5, 1: 0.0, 2: 0.0}
AHEAD = 1.5
ISSUE, MULTIPLY = 0.08, (0.4, 1.0)
RANK = {0: 0, 3: 1, 1: 2, 2: 3}
LINKS = {
    "e": "a00- b000 b001 a030 b030 b300 b301 b330 b100 b101 b130 b200 b201 b230",
    "w": "a00- b001 b000 a011 b011 b300 b301 b101 b311 b100 b111 b201 b200 b211",
    "n": "b000 b001 a00- b300 a03- a01- a020 a021 a300 a330 a310 a320",
    "s": "b001 b000 a00- b101 a01- a03- a021 a020 a101 a111 a131 a121",
}


def moved(dy, dx, to):
    sy, sx = {"n": (-1, 0), "s": (1, 0), "e": (0, -1), "w": (0, 1)}[to]
    return (dy + sy) % NY, (dx + sx) % NX


def steps():
    found = []
    for to, names in LINKS.items():
        axis = "y" if to in "ns" else "x"
        for n, name in enumerate(names.split()):
            kind, dy, dx = name[0], int(name[1]), int(name[2])
            h = None if name[3] == "-" else int(name[3])
            needs = () if dy == dx == 0 else ((kind, dy, dx, h),)
            if n:
                needs += (("queued", to, n - 1),)
            held = HOLDS[kind, axis] * (2 if h is None else 1)
            found.append((n, needs, axis + to, held, (kind, *moved(dy, dx, to), h), ("go", kind, dy, dx, h, to)))
    found.append((0, (), "", 0.0, "tok", ("tok",)))
    for g in range(NY):
        for k, kind in enumerate("ab"):
            needs = [step[4] for step in found if step[4][:2] == (kind, g)]
            needs += ["local", "tok " + kind]
            found.append((60 + RANK[g], tuple(needs), "", MULTIPLY[k], ("mul", g, k), ("mul", g, k)))
            for n, (sign, hops, _) in enumerate(ARCS[k]):
                for t in range(hops):
                    needs = (("mul", g, k),) + ((("ring", g, k, n, t - 1),) if t else ())
                    sent = ("ring", g, k, n, t)
                    found.append((40 + RANK[g] - t / 8, needs, "z+" if sign > 0 else "z-", SUM_HOLDS, sent, ("add", g, k, n, t)))
            needs = tuple(("ring", g, k, n, hops - 1) for n, (_, hops, _) in enumerate(ARCS[k]))
            if k:
                found.append((50 + RANK[g], needs, "c", SUM_HOLDS, ("cross", g), ("cross", g)))
            else:
                found.append((51 + RANK[g], needs, "", 0.1, ("keep", g), ("keep", g)))
        found.append((55 + RANK[g], (("cross", g), ("keep", g)), "", 0.1, ("score", g), ("score", g)))
    names = {step[4] for step in found} | {"local", "tok a", "tok b"}
    whole = lambda name: name if name in names or name[0] == "queued" else (*name[:3], None)
    return [(order, tuple(map(whole, needs)), *rest) for order, needs, *rest in found]


def ordered():
    left, arrives, free, now, seen, order = steps(), {"local": 4.0}, {}, 0.0, set(), []
    here = ("mul", "keep", "score", "queued")
    while left:
        best = None
        for step in left:
            if all(name in arrives for name in step[1]):
                ready = max([now] + [arrives[name] for name in step[1]])
                if step[2][:1] == "y":
                    ready = max(ready, free.get(step[2], 0.0) - AHEAD)
                if best is None or (ready, step[0]) < best[0]:
                    best = ((ready, step[0]), step)
        (ready, n), step = best
        left.remove(step)
        _, needs, link, held, sent, what = step
        order.append((tuple(name for name in needs if name not in seen and name[0] not in here), what))
        seen.update(needs)
        if link:
            now = ready + ISSUE
            free[link] = max(now, free.get(link, 0.0)) + held
            arrives[sent] = free[link] + LATENCY[link[0]] + (SLACK[sent[1]] if sent[0] == "ring" else 0.0)
            if what[0] == "go":
                arrives["queued", link[1], n] = now
        elif sent == "tok":
            now = ready + ISSUE
            arrives["tok b"], arrives["tok a"] = now + 6.0, now + 8.0
        else:
            now = arrives[sent] = ready + held
        TIMES.append((now, what))
    return order


TIMES = []


class Plan:
    def __init__(self, send_sem, recv_sem):
        self.send_sem, self.recv_sem, self.copies = send_sem, recv_sem, {}

    def send(self, name, src, dst, device):
        n = len(self.copies)
        assert n < COPIES
        copy = pltpu.make_async_remote_copy(
            src_ref=src,
            dst_ref=dst,
            send_sem=self.send_sem.at[n],
            recv_sem=self.recv_sem.at[n],
            device_id=device,
            device_id_type=MESH,
        )
        copy.start()
        self.copies[name] = copy

    def arrived(self, name, dst=None):
        if dst is None:
            self.copies[name].wait_recv()
            return
        n = list(self.copies).index(name)
        pltpu.make_async_remote_copy(
            src_ref=dst,
            dst_ref=dst,
            send_sem=self.send_sem.at[n],
            recv_sem=self.recv_sem.at[n],
            device_id={"tensor": lax.axis_index("tensor")},
            device_id_type=MESH,
        ).wait_recv()

    def drain(self):
        for copy in self.copies.values():
            copy.wait_send()


def kernel(
    own_ref, out_ref, vown_ref, vout_ref,
    tokens_ref, seq_ref,
    tok_a, tok_b, val_a, val_b, part, hop, kept, cross, got, tile, tiles,
    local_sem, send_sem, recv_sem,
):
    d, sec, z = lax.axis_index("dp"), lax.axis_index("section"), lax.axis_index("tensor")
    core, x, y = d % 2, (d // 2) % NX, d // (2 * NX)
    rows, share = own_ref.shape[0], vown_ref.shape[0]
    half, block = share // 2, rows // NZ

    def at(yy, xx, cc):
        return {"dp": (yy * NX + xx) * 2 + cc}

    east, west = at(y, (x + 1) % NX, core), at(y, (x + NX - 1) % NX, core)
    north, south = at((y + 1) % NY, x, core), at((y + NY - 1) % NY, x, core)
    sibling = at(y, x, 1 - core)
    partner = {"section": 1 - sec}
    diagonal = {"dp": sibling["dp"], "section": 1 - sec}
    up, down = {"tensor": (z + 1) % NZ}, {"tensor": (z + NZ - 1) % NZ}

    barrier = pltpu.get_barrier_semaphore()
    greeted = (east, west, north, south, sibling, partner, diagonal, up, down)
    for device in greeted:
        pl.semaphore_signal(barrier, inc=1, device_id=device, device_id_type=MESH)

    local = [
        pltpu.make_async_copy(vout_ref, val_b.at[0, pl.ds(0, share)], local_sem.at[0]),
        pltpu.make_async_copy(vown_ref, val_a.at[0, pl.ds(0, share)], local_sem.at[1]),
        pltpu.make_async_copy(out_ref, tok_b.at[pl.ds(0, rows)], local_sem.at[2]),
        pltpu.make_async_copy(own_ref, tok_a.at[pl.ds(0, rows)], local_sem.at[3]),
    ]
    for copy in local:
        copy.start()
    pl.semaphore_wait(barrier, len(greeted))

    plan = Plan(send_sem, recv_sem)

    def slot(kind, dy, dx, h=None):
        ref = val_a if kind == "a" else val_b
        first, count = (dx * share, share) if h is None else (dx * share + h * half, half)
        return ref.at[dy, pl.ds(first, count)]

    def go(kind, dy, dx, h, to):
        device = {"n": north, "s": south, "e": east, "w": west}[to]
        ty, tx = moved(dy, dx, to)
        src = slot(kind, dy, dx, h)
        if dy == dx == 0:
            ref = vown_ref if kind == "a" else vout_ref
            src = ref if h is None else ref.at[pl.ds(h * half, half)]
        plan.send((kind, ty, tx, h), src, slot(kind, ty, tx, h), device)

    def multiply(g, k):
        tok, val = ((tok_a, val_a), (tok_b, val_b))[k]
        for c in range(2):
            gram = lax.dot_general(
                tok[pl.ds(c * rows, rows), :], val[g], (((1,), (1,)), ((), ())), preferred_element_type=jnp.float32
            )
            part[g, k, :, pl.ds(c * block, block), :] = gram.reshape(NZ, block, NX * share)

    def add_up(g, k, n, t):
        sign, steps, base = ARCS[k][n]
        owner = (z + NZ + sign * (steps - t)) % NZ
        src = part.at[g, k, owner]
        if t:
            src = hop.at[g, base + t - 1]
            src[...] = src[...] + part[g, k, owner]
        plan.send(("ring", g, k, n, t), src, hop.at[g, base + t], up if sign > 0 else down)

    def reduced(g, k):
        total = part[g, k, z]
        for _, steps, base in ARCS[k]:
            total = total + hop[g, base + steps - 1]
        return total

    first = True
    for needs, (what, *at_) in ordered():
        for name in needs:
            if name == "local":
                for copy in local:
                    copy.wait()
            else:
                plan.arrived(name)
        if what == "go":
            go(*at_)
        elif what == "tok":
            plan.send("tok b", out_ref, tok_b.at[pl.ds(rows, rows)], sibling)
            plan.send("tok a", own_ref, tok_a.at[pl.ds(rows, rows)], sibling)
        elif what == "mul":
            multiply(*at_)
        elif what == "add":
            add_up(*at_)
        elif what == "keep":
            kept[at_[0]] = reduced(at_[0], 0)
        elif what == "cross":
            cross[at_[0]] = reduced(at_[0], 1)
            plan.send(("cross", at_[0]), cross.at[at_[0]], got.at[at_[0]], partner)
        elif what == "score":
            term = kept[at_[0]] * got[at_[0]]
            total, first = (term if first else total + term), False

    scores = jnp.sum(total.T, axis=0, keepdims=True)
    tile[...] = jnp.zeros_like(tile)
    tile[0:1, 0:block] = scores[:, 0:block]
    tile[1:2, 0:block] = scores[:, block:]
    near = ({}, partner, sibling, diagonal)
    tiles[z, 0] = tile[...]
    for r in (4, 3, 5, 2, 6, 1, 7, 0):
        for j in range(4):
            if r or j:
                plan.send(("end", r, j), tile, tiles.at[z, j], {**near[j], "tensor": (z + r) % NZ})
    for r in (0, 1, 7, 2, 6, 3, 5, 4):
        for j in range(4):
            if r or j:
                plan.arrived(("end", r, j), tiles.at[(z + NZ - r) % NZ, j])
    tokens_ref[...] = ((tiles[z, 0, 0:1] + tiles[z, 1, 0:1]) + (tiles[z, 2, 1:2] + tiles[z, 3, 1:2]))[:, 0:block]
    every = (tiles[:, 0, 0:1] + tiles[:, 1, 0:1]) + (tiles[:, 2, 1:2] + tiles[:, 3, 1:2])
    seq_ref[...] = jnp.sum(jnp.sum(every, axis=0), axis=1, keepdims=True)
    plan.drain()


COPIES = 160


def body(own_rows, out_rows, val_own, val_out):
    rows, wide_a = own_rows.shape[1:]
    share, wide_b = val_out.shape[1:]
    block, group = rows // NZ, NX * share
    f32, bf16 = jnp.float32, jnp.bfloat16
    hbm = pl.BlockSpec(memory_space=pl.ANY)
    vmem = pl.BlockSpec(memory_space=pltpu.VMEM)
    tokens, seq = pl.pallas_call(
        kernel,
        out_shape=(pltpu.VMEM((1, block), f32), pltpu.VMEM((1, 1), f32)),
        in_specs=[hbm] * 4,
        out_specs=(vmem, vmem),
        scratch_shapes=[
            pltpu.VMEM((2 * rows, wide_a), bf16),
            pltpu.VMEM((2 * rows, wide_b), bf16),
            pltpu.VMEM((NY, group, wide_a), bf16),
            pltpu.VMEM((NY, group, wide_b), bf16),
            pltpu.VMEM((NY, 2, NZ, 2 * block, group), f32),
            pltpu.VMEM((NY, 14, 2 * block, group), f32),
            pltpu.VMEM((NY, 2 * block, group), f32),
            pltpu.VMEM((NY, 2 * block, group), f32),
            pltpu.VMEM((NY, 2 * block, group), f32),
            pltpu.VMEM((8, 128), f32),
            pltpu.VMEM((NZ, 4, 8, 128), f32),
            pltpu.SemaphoreType.DMA((4,)),
            pltpu.SemaphoreType.DMA((COPIES,)),
            pltpu.SemaphoreType.DMA((COPIES,)),
        ],
        compiler_params=pltpu.CompilerParams(
            collective_id=0, has_side_effects=True, vmem_limit_bytes=62 * 1024 * 1024
        ),
    )(own_rows[0], out_rows[0], val_own[0], val_out[0])
    return tokens.reshape(block), seq.reshape(1)


def solution(mesh):
    spec = P("section", "dp", "tensor")
    return jax.shard_map(
        body,
        mesh=mesh,
        in_specs=(spec,) * 4,
        out_specs=(P(("dp", "tensor")), P("dp")),
        check_vma=False,
    )
```

```python
import jax
import jax.numpy as jnp
from jax import lax
from jax.experimental import pallas as pl
from jax.experimental.pallas import tpu as pltpu
from jax.sharding import PartitionSpec as P

NX = 4
NY = 4
NZ = 8
MESH = pl.DeviceIdType.MESH


ARCS = (((-1, 4, 0), (1, 3, 4)), ((1, 4, 7), (-1, 3, 11)))
HOLDS = {("a", "x"): 0.7, ("a", "y"): 1.41, ("b", "x"): 2.47, ("b", "y"): 4.93}
SUM_HOLDS = 0.7
LATENCY = {"x": 2.0, "y": 3.0, "z": 1.8, "c": 1.8}
SLACK = {0: 4.0, 3: 0.5, 1: 0.0, 2: 0.0}
AHEAD = 1.5
ISSUE, MULTIPLY = 0.08, (0.4, 1.0)
RANK = {0: 0, 3: 1, 1: 2, 2: 3}
LINKS = {
    "e": ("a00-", "b000", "b001", "a030", "b030", "b300", "b301", "b330", "b100", "b101", "b130", "b200", "b201", "b230"),
    "w": ("a00-", "b001", "b000", "a011", "b011", "b300", "b301", "b101", "b311", "b100", "b111", "b201", "b200", "b211"),
    "n": ("b000", "b001", "a00-", "b300", "a03-", "a01-", "a020", "a021", "a300", "a330", "a310", "a320"),
    "s": ("b001", "b000", "a00-", "b101", "a01-", "a03-", "a021", "a020", "a101", "a111", "a131", "a121"),
}


def moved(dy, dx, to):
    sy, sx = {"n": (-1, 0), "s": (1, 0), "e": (0, -1), "w": (0, 1)}[to]
    return (dy + sy) % NY, (dx + sx) % NX


def steps():
    found = []
    for to, names in LINKS.items():
        axis = "y" if to in "ns" else "x"
        for n, name in enumerate(names):
            kind, dy, dx = name[0], int(name[1]), int(name[2])
            h = None if name[3] == "-" else int(name[3])
            needs = () if dy == dx == 0 else ((kind, dy, dx, h),)
            if n:
                needs += (("queued", to, n - 1),)
            held = HOLDS[kind, axis] * (2 if h is None else 1)
            found.append((n, needs, axis + to, held, (kind, *moved(dy, dx, to), h), ("go", kind, dy, dx, h, to)))
    found.append((0, (), "", 0.0, "tok", ("tok",)))
    for g in range(NY):
        for k, kind in enumerate("ab"):
            needs = [step[4] for step in found if step[4][:2] == (kind, g)]
            needs += ["local", "tok " + kind]
            found.append((60 + RANK[g], tuple(needs), "", MULTIPLY[k], ("mul", g, k), ("mul", g, k)))
            for n, (sign, hops, _) in enumerate(ARCS[k]):
                for t in range(hops):
                    needs = (("mul", g, k),) + ((("ring", g, k, n, t - 1),) if t else ())
                    sent = ("ring", g, k, n, t)
                    found.append((40 + RANK[g] - t / 8, needs, "z+" if sign > 0 else "z-", SUM_HOLDS, sent, ("add", g, k, n, t)))
            needs = tuple(("ring", g, k, n, hops - 1) for n, (_, hops, _) in enumerate(ARCS[k]))
            if k:
                found.append((50 + RANK[g], needs, "c", SUM_HOLDS, ("cross", g), ("cross", g)))
            else:
                found.append((51 + RANK[g], needs, "", 0.1, ("keep", g), ("keep", g)))
        found.append((55 + RANK[g], (("cross", g), ("keep", g)), "", 0.1, ("score", g), ("score", g)))
    names = {step[4] for step in found} | {"local", "tok a", "tok b"}
    whole = lambda name: name if name in names or name[0] == "queued" else (*name[:3], None)
    return [(order, tuple(map(whole, needs)), *rest) for order, needs, *rest in found]


def ordered():
    left, arrives, free, now, seen, order = steps(), {"local": 4.0}, {}, 0.0, set(), []
    here = ("mul", "keep", "score", "queued")
    while left:
        best = None
        for step in left:
            if all(name in arrives for name in step[1]):
                ready = max([now] + [arrives[name] for name in step[1]])
                if step[2][:1] == "y":
                    ready = max(ready, free.get(step[2], 0.0) - AHEAD)
                if best is None or (ready, step[0]) < best[0]:
                    best = ((ready, step[0]), step)
        (ready, n), step = best
        left.remove(step)
        _, needs, link, held, sent, what = step
        order.append((tuple(name for name in needs if name not in seen and name[0] not in here), what))
        seen.update(needs)
        if link:
            now = ready + ISSUE
            free[link] = max(now, free.get(link, 0.0)) + held
            arrives[sent] = free[link] + LATENCY[link[0]] + (SLACK[sent[1]] if sent[0] == "ring" else 0.0)
            if what[0] == "go":
                arrives["queued", link[1], n] = now
        elif sent == "tok":
            now = ready + ISSUE
            arrives["tok b"], arrives["tok a"] = now + 6.0, now + 8.0
        else:
            now = arrives[sent] = ready + held
        TIMES.append((now, what))
    return order


TIMES = []


def together(name):
    what, *at_ = name if isinstance(name, tuple) else (name,)
    if what == "b" and (at_[1] == 2 or (at_[1], at_[2]) in ((NX - 1, 1), (1, 0))):
        return ("row b", at_[0])
    if what == "a" and at_[0] == 2:
        return ("row a",)
    if what == "ring" and at_[3] == ARCS[at_[1]][at_[2]][1] - 1:
        return ("sum", at_[0], at_[1])
    if what == "end":
        return ("end",)
    return name


class Plan:
    def __init__(self, send_sem, recv_sem, sent, landed):
        self.send_sem, self.recv_sem, self.sent, self.landed = send_sem, recv_sem, sent, landed
        self.copies, self.sems, self.waited = {}, {}, set()

    def send(self, name, src, dst, device):
        what = name[0] if isinstance(name, tuple) else name
        n = self.sems.setdefault(together(name), len(self.sems))
        assert n < ARRIVALS
        copy = pltpu.make_async_remote_copy(
            src_ref=src,
            dst_ref=dst,
            send_sem=self.send_sem.at[list(self.sent).index(what)],
            recv_sem=self.recv_sem.at[n],
            device_id=device,
            device_id_type=MESH,
        )
        copy.start()
        self.copies[name] = copy

    def bytes_of(self, ref, send, recv):
        return pltpu.make_async_remote_copy(
            src_ref=ref,
            dst_ref=ref,
            send_sem=self.send_sem.at[send],
            recv_sem=self.recv_sem.at[recv],
            device_id={"tensor": lax.axis_index("tensor")},
            device_id_type=MESH,
        )

    def arrived(self, name):
        key = together(name)
        if key in self.waited:
            return
        self.waited.add(key)
        if key == name:
            self.copies[name].wait_recv()
        else:
            self.bytes_of(self.landed[key[0]], 0, self.sems[key]).wait_recv()

    def drain(self):
        for n, ref in enumerate(self.sent.values()):
            self.bytes_of(ref, n, 0).wait_send()


def kernel(
    own_ref, out_ref, vown_ref, vout_ref,
    tokens_ref, seq_ref,
    tok_a, tok_b, val_a, val_b, part, hop, kept, cross, got, tile, tiles,
    local_sem, send_sem, recv_sem,
):
    d, sec, z = lax.axis_index("dp"), lax.axis_index("section"), lax.axis_index("tensor")
    core, x, y = d % 2, (d // 2) % NX, d // (2 * NX)
    rows, share = own_ref.shape[0], vown_ref.shape[0]
    half, block = share // 2, rows // NZ

    def at(yy, xx, cc):
        return {"dp": (yy * NX + xx) * 2 + cc}

    east, west = at(y, (x + 1) % NX, core), at(y, (x + NX - 1) % NX, core)
    north, south = at((y + 1) % NY, x, core), at((y + NY - 1) % NY, x, core)
    sibling = at(y, x, 1 - core)
    partner = {"section": 1 - sec}
    diagonal = {"dp": sibling["dp"], "section": 1 - sec}
    up, down = {"tensor": (z + 1) % NZ}, {"tensor": (z + NZ - 1) % NZ}

    barrier = pltpu.get_barrier_semaphore()
    greeted = (east, west, north, south, sibling, partner, diagonal, up, down)
    for device in greeted:
        pl.semaphore_signal(barrier, inc=1, device_id=device, device_id_type=MESH)

    local = [
        pltpu.make_async_copy(vout_ref, val_b.at[0, pl.ds(0, share)], local_sem.at[0]),
        pltpu.make_async_copy(vown_ref, val_a.at[0, pl.ds(0, share)], local_sem.at[1]),
        pltpu.make_async_copy(out_ref, tok_b.at[pl.ds(0, rows)], local_sem.at[2]),
        pltpu.make_async_copy(own_ref, tok_a.at[pl.ds(0, rows)], local_sem.at[3]),
    ]
    for copy in local:
        copy.start()
    pl.semaphore_wait(barrier, len(greeted))

    count = {}
    for to in LINKS:
        for name in LINKS[to]:
            count[name[0]] = count.get(name[0], 0) + (share if name[3] == "-" else half)
    sent = {
        "a": tok_a.at[pl.ds(0, count["a"])],
        "b": tok_b.at[pl.ds(0, count["b"])],
        "tok a": own_ref,
        "tok b": out_ref,
        "ring": hop,
        "cross": cross,
        "end": tiles.at[pl.ds(0, 4 * NZ - 1)],
    }
    landed = {
        "row a": val_a.at[0],
        "row b": val_b.at[0, pl.ds(0, 4 * half)],
        "sum": hop.at[0, pl.ds(0, 2)],
        "end": tiles.at[pl.ds(0, 4 * NZ - 1)],
    }
    plan = Plan(send_sem, recv_sem, sent, landed)

    def slot(kind, dy, dx, h=None):
        ref = val_a if kind == "a" else val_b
        first, count = (dx * share, share) if h is None else (dx * share + h * half, half)
        return ref.at[dy, pl.ds(first, count)]

    def go(kind, dy, dx, h, to):
        device = {"n": north, "s": south, "e": east, "w": west}[to]
        ty, tx = moved(dy, dx, to)
        src = slot(kind, dy, dx, h)
        if dy == dx == 0:
            ref = vown_ref if kind == "a" else vout_ref
            src = ref if h is None else ref.at[pl.ds(h * half, half)]
        plan.send((kind, ty, tx, h), src, slot(kind, ty, tx, h), device)

    def multiply(g, k):
        tok, val = ((tok_a, val_a), (tok_b, val_b))[k]
        for c in range(2):
            gram = lax.dot_general(
                tok[pl.ds(c * rows, rows), :], val[g], (((1,), (1,)), ((), ())), preferred_element_type=jnp.float32
            )
            part[g, k, :, pl.ds(c * block, block), :] = gram.reshape(NZ, block, NX * share)

    def add_up(g, k, n, t):
        sign, steps, base = ARCS[k][n]
        owner = (z + NZ + sign * (steps - t)) % NZ
        src = part.at[g, k, owner]
        if t:
            src = hop.at[g, base + t - 1]
            src[...] = src[...] + part[g, k, owner]
        plan.send(("ring", g, k, n, t), src, hop.at[g, base + t], up if sign > 0 else down)

    def reduced(g, k):
        total = part[g, k, z]
        for _, steps, base in ARCS[k]:
            total = total + hop[g, base + steps - 1]
        return total

    first = True
    for needs, (what, *at_) in ordered():
        for name in needs:
            if name == "local":
                for copy in local:
                    copy.wait()
            else:
                plan.arrived(name)
        if what == "go":
            go(*at_)
        elif what == "tok":
            plan.send("tok b", out_ref, tok_b.at[pl.ds(rows, rows)], sibling)
            plan.send("tok a", own_ref, tok_a.at[pl.ds(rows, rows)], sibling)
        elif what == "mul":
            multiply(*at_)
        elif what == "add":
            add_up(*at_)
        elif what == "keep":
            kept[at_[0]] = reduced(at_[0], 0)
        elif what == "cross":
            cross[at_[0]] = reduced(at_[0], 1)
            plan.send(("cross", at_[0]), cross.at[at_[0]], got.at[at_[0]], partner)
        elif what == "score":
            term = kept[at_[0]] * got[at_[0]]
            total, first = (term if first else total + term), False

    scores = jnp.sum(total.T, axis=0, keepdims=True)
    tile[...] = jnp.zeros_like(tile)
    tile[0:1, 0:block] = scores[:, 0:block]
    tile[1:2, 0:block] = scores[:, block:]
    near = ({}, partner, sibling, diagonal)
    tiles[4 * z] = tile[...]
    for r in (4, 3, 5, 2, 6, 1, 7, 0):
        for j in range(4):
            if r or j:
                plan.send(("end", r, j), tile, tiles.at[4 * z + j], {**near[j], "tensor": (z + r) % NZ})
    plan.arrived(("end", 1, 0))
    tokens_ref[...] = (
        (tiles[4 * z, 0:1] + tiles[4 * z + 1, 0:1]) + (tiles[4 * z + 2, 1:2] + tiles[4 * z + 3, 1:2])
    )[:, 0:block]
    every = jnp.zeros_like(tiles[0, 0:1])
    for r in range(NZ):
        every = every + (
            (tiles[4 * r, 0:1] + tiles[4 * r + 1, 0:1]) + (tiles[4 * r + 2, 1:2] + tiles[4 * r + 3, 1:2])
        )
    seq_ref[...] = jnp.sum(every, axis=1, keepdims=True)
    plan.drain()
    assert len(plan.sems) == ARRIVALS


ARRIVALS = 88


def body(own_rows, out_rows, val_own, val_out):
    rows, wide_a = own_rows.shape[1:]
    share, wide_b = val_out.shape[1:]
    block, group = rows // NZ, NX * share
    f32, bf16 = jnp.float32, jnp.bfloat16
    hbm = pl.BlockSpec(memory_space=pl.ANY)
    vmem = pl.BlockSpec(memory_space=pltpu.VMEM)
    tokens, seq = pl.pallas_call(
        kernel,
        out_shape=(pltpu.VMEM((1, block), f32), pltpu.VMEM((1, 1), f32)),
        in_specs=[hbm] * 4,
        out_specs=(vmem, vmem),
        scratch_shapes=[
            pltpu.VMEM((2 * rows, wide_a), bf16),
            pltpu.VMEM((2 * rows, wide_b), bf16),
            pltpu.VMEM((NY, group, wide_a), bf16),
            pltpu.VMEM((NY, group, wide_b), bf16),
            pltpu.VMEM((NY, 2, NZ, 2 * block, group), f32),
            pltpu.VMEM((NY, 14, 2 * block, group), f32),
            pltpu.VMEM((NY, 2 * block, group), f32),
            pltpu.VMEM((NY, 2 * block, group), f32),
            pltpu.VMEM((NY, 2 * block, group), f32),
            pltpu.VMEM((8, 128), f32),
            pltpu.VMEM((4 * NZ, 8, 128), f32),
            pltpu.SemaphoreType.DMA((4,)),
            pltpu.SemaphoreType.DMA((7,)),
            pltpu.SemaphoreType.DMA((ARRIVALS,)),
        ],
        compiler_params=pltpu.CompilerParams(
            collective_id=0, has_side_effects=True, vmem_limit_bytes=62 * 1024 * 1024
        ),
    )(own_rows[0], out_rows[0], val_own[0], val_out[0])
    return tokens.reshape(block), seq.reshape(1)


def solution(mesh):
    spec = P("section", "dp", "tensor")
    return jax.shard_map(
        body,
        mesh=mesh,
        in_specs=(spec,) * 4,
        out_specs=(P(("dp", "tensor")), P("dp")),
        check_vma=False,
    )
```

```python
import jax
import jax.numpy as jnp
from jax import lax
from jax.experimental import pallas as pl
from jax.experimental.pallas import tpu as pltpu
from jax.sharding import PartitionSpec as P

NX = 4
NY = 4
NZ = 8
MESH = pl.DeviceIdType.MESH


ARCS = (((-1, 4, 0), (1, 3, 4)), ((1, 4, 7), (-1, 3, 11)))
HOLDS = {("a", "x"): 0.7, ("a", "y"): 1.41, ("b", "x"): 2.47, ("b", "y"): 4.93}
SUM_HOLDS = 0.7
LATENCY = {"x": 2.0, "y": 3.0, "z": 1.8, "c": 1.8}
SLACK = {0: 1.0, 3: 0.5, 1: 0.0, 2: 0.0}
AHEAD = 1.5
ISSUE, MULTIPLY = 0.08, (0.4, 1.0)
RANK = {0: 0, 3: 1, 1: 1, 2: 0}
LAST = 2
LINKS = {
    "e": ("a00-", "b000", "b001", "a030", "b030", "b300", "b301", "b330", "b100", "b101", "b130", "b200", "b201", "b230"),
    "w": ("a00-", "b001", "b000", "a011", "b011", "b300", "b301", "b101", "b311", "b100", "b111", "b201", "b200", "b211"),
    "n": ("b000", "b001", "a00-", "b300", "a03-", "a01-", "a020", "a021", "a300", "a330", "a310", "a320"),
    "s": ("b001", "b000", "a00-", "b101", "a01-", "a03-", "a021", "a020", "a101", "a111", "a131", "a121"),
}


def moved(dy, dx, to):
    sy, sx = {"n": (-1, 0), "s": (1, 0), "e": (0, -1), "w": (0, 1)}[to]
    return (dy + sy) % NY, (dx + sx) % NX


def steps():
    found = []
    for to, names in LINKS.items():
        axis = "y" if to in "ns" else "x"
        for n, name in enumerate(names):
            kind, dy, dx = name[0], int(name[1]), int(name[2])
            h = None if name[3] == "-" else int(name[3])
            needs = () if dy == dx == 0 else ((kind, dy, dx, h),)
            if n:
                needs += (("queued", to, n - 1),)
            held = HOLDS[kind, axis] * (2 if h is None else 1)
            found.append((n, needs, axis + to, held, (kind, *moved(dy, dx, to), h), ("go", kind, dy, dx, h, to)))
    found.append((0, (), "", 0.0, "tok", ("tok",)))
    for g in range(NY):
        for k, kind in enumerate("ab"):
            needs = [step[4] for step in found if step[4][:2] == (kind, g)]
            needs += ["local", "tok " + kind]
            found.append((60 + RANK[g], tuple(needs), "", MULTIPLY[k], ("mul", g, k), ("mul", g, k)))
            for n, (sign, hops, _) in enumerate(ARCS[k]):
                for t in range(hops):
                    stride = 2 if g == LAST else 1
                    needs = (("mul", g, k),) + ((("ring", g, k, n, t - stride),) if t >= stride else ())
                    if g == LAST:
                        needs += (("keep", 0), ("cross", 0))
                    sent = ("ring", g, k, n, t)
                    found.append((40 + RANK[g] - t / 8, needs, "z+" if sign > 0 else "z-", SUM_HOLDS, sent, ("add", g, k, n, t)))
            needs = tuple(("ring", g, k, n, hops - 1) for n, (_, hops, _) in enumerate(ARCS[k]))
            if g == LAST:
                needs += tuple(("ring", g, k, n, hops - 2) for n, (_, hops, _) in enumerate(ARCS[k]))
            if k and g == LAST:
                found.append((40, (("mul", g, k),), "c", SUM_HOLDS, ("cross", g), ("give",)))
                last = needs
            elif k:
                found.append((50 + RANK[g], needs, "c", SUM_HOLDS, ("cross", g), ("cross", g)))
            else:
                found.append((51 + RANK[g], needs, "", 0.1, ("keep", g), ("keep", g)))
        needs = (("cross", g), ("keep", g)) + (last if g == LAST else ())
        found.append((55 + RANK[g], needs, "", 0.1, ("score", g), ("score", g)))
    names = {step[4] for step in found} | {"local", "tok a", "tok b"}
    whole = lambda name: name if name in names or name[0] == "queued" else (*name[:3], None)
    return [(order, tuple(map(whole, needs)), *rest) for order, needs, *rest in found]


def ordered():
    left, arrives, free, now, seen, order = steps(), {"local": 4.0}, {}, 0.0, set(), []
    here = ("mul", "keep", "score", "queued")
    while left:
        best = None
        for step in left:
            if all(name in arrives for name in step[1]):
                ready = max([now] + [arrives[name] for name in step[1]])
                if step[2][:1] == "y":
                    ready = max(ready, free.get(step[2], 0.0) - AHEAD)
                if best is None or (ready, step[0]) < best[0]:
                    best = ((ready, step[0]), step)
        (ready, n), step = best
        left.remove(step)
        _, needs, link, held, sent, what = step
        order.append((tuple(name for name in needs if name not in seen and name[0] not in here), what))
        seen.update(needs)
        if link:
            now = ready + ISSUE
            free[link] = max(now, free.get(link, 0.0)) + held
            arrives[sent] = free[link] + LATENCY[link[0]] + (SLACK[sent[1]] if sent[0] == "ring" else 0.0)
            if what[0] == "go":
                arrives["queued", link[1], n] = now
        elif sent == "tok":
            now = ready + ISSUE
            arrives["tok b"], arrives["tok a"] = now + 6.0, now + 8.0
        else:
            now = arrives[sent] = ready + held
        TIMES.append((now, what))
    return order


TIMES = []


def together(name):
    what, *at_ = name if isinstance(name, tuple) else (name,)
    if what == "b" and (at_[1] == 2 or (at_[1], at_[2]) in ((NX - 1, 1), (1, 0))):
        return ("row b", at_[0])
    if what == "a" and at_[0] == 2:
        return ("row a",)
    if what == "ring" and at_[3] >= ARCS[at_[1]][at_[2]][1] - (2 if at_[0] == LAST else 1):
        return ("last sum" if at_[0] == LAST else "sum", at_[0], at_[1])
    if what == "end":
        return ("end",)
    return name


class Plan:
    def __init__(self, send_sem, recv_sem, sent, landed):
        self.send_sem, self.recv_sem, self.sent, self.landed = send_sem, recv_sem, sent, landed
        self.copies, self.sems, self.waited = {}, {}, set()

    def send(self, name, src, dst, device):
        what = name[0] if isinstance(name, tuple) else name
        n = self.sems.setdefault(together(name), len(self.sems))
        assert n < ARRIVALS
        copy = pltpu.make_async_remote_copy(
            src_ref=src,
            dst_ref=dst,
            send_sem=self.send_sem.at[list(self.sent).index(what)],
            recv_sem=self.recv_sem.at[n],
            device_id=device,
            device_id_type=MESH,
        )
        copy.start()
        self.copies[name] = copy

    def bytes_of(self, ref, send, recv):
        return pltpu.make_async_remote_copy(
            src_ref=ref,
            dst_ref=ref,
            send_sem=self.send_sem.at[send],
            recv_sem=self.recv_sem.at[recv],
            device_id={"tensor": lax.axis_index("tensor")},
            device_id_type=MESH,
        )

    def arrived(self, name):
        key = together(name)
        if key in self.waited:
            return
        self.waited.add(key)
        if key == name:
            self.copies[name].wait_recv()
        else:
            self.bytes_of(self.landed[key[0]], 0, self.sems[key]).wait_recv()

    def drain(self):
        for n, ref in enumerate(self.sent.values()):
            self.bytes_of(ref, n, 0).wait_send()


def kernel(
    own_ref, out_ref, vown_ref, vout_ref,
    tokens_ref, seq_ref,
    tok_a, tok_b, val_a, val_b, part, hop, kept, cross, got, tile, tiles,
    local_sem, send_sem, recv_sem,
):
    d, sec, z = lax.axis_index("dp"), lax.axis_index("section"), lax.axis_index("tensor")
    core, x, y = d % 2, (d // 2) % NX, d // (2 * NX)
    rows, share = own_ref.shape[0], vown_ref.shape[0]
    half, block = share // 2, rows // NZ

    def at(yy, xx, cc):
        return {"dp": (yy * NX + xx) * 2 + cc}

    east, west = at(y, (x + 1) % NX, core), at(y, (x + NX - 1) % NX, core)
    north, south = at((y + 1) % NY, x, core), at((y + NY - 1) % NY, x, core)
    sibling = at(y, x, 1 - core)
    partner = {"section": 1 - sec}
    diagonal = {"dp": sibling["dp"], "section": 1 - sec}
    up, down = {"tensor": (z + 1) % NZ}, {"tensor": (z + NZ - 1) % NZ}

    barrier = pltpu.get_barrier_semaphore()
    greeted = (east, west, north, south, sibling, partner, diagonal, up, down)
    for device in greeted:
        pl.semaphore_signal(barrier, inc=1, device_id=device, device_id_type=MESH)

    local = [
        pltpu.make_async_copy(vout_ref, val_b.at[0, pl.ds(0, share)], local_sem.at[0]),
        pltpu.make_async_copy(vown_ref, val_a.at[0, pl.ds(0, share)], local_sem.at[1]),
        pltpu.make_async_copy(out_ref, tok_b.at[pl.ds(0, rows)], local_sem.at[2]),
        pltpu.make_async_copy(own_ref, tok_a.at[pl.ds(0, rows)], local_sem.at[3]),
    ]
    for copy in local:
        copy.start()
    pl.semaphore_wait(barrier, len(greeted))

    count = {}
    for to in LINKS:
        for name in LINKS[to]:
            count[name[0]] = count.get(name[0], 0) + (share if name[3] == "-" else half)
    sent = {
        "a": tok_a.at[pl.ds(0, count["a"])],
        "b": tok_b.at[pl.ds(0, count["b"])],
        "tok a": own_ref,
        "tok b": out_ref,
        "ring": hop,
        "cross": cross,
        "end": tiles.at[pl.ds(0, 4 * NZ - 1)],
    }
    landed = {
        "row a": val_a.at[0],
        "row b": val_b.at[0, pl.ds(0, 4 * half)],
        "sum": hop.at[0, pl.ds(0, 2)],
        "last sum": hop.at[0, pl.ds(0, 4)],
        "end": tiles.at[pl.ds(0, 4 * NZ - 1)],
    }
    plan = Plan(send_sem, recv_sem, sent, landed)

    def slot(kind, dy, dx, h=None):
        ref = val_a if kind == "a" else val_b
        first, count = (dx * share, share) if h is None else (dx * share + h * half, half)
        return ref.at[dy, pl.ds(first, count)]

    def go(kind, dy, dx, h, to):
        device = {"n": north, "s": south, "e": east, "w": west}[to]
        ty, tx = moved(dy, dx, to)
        src = slot(kind, dy, dx, h)
        if dy == dx == 0:
            ref = vown_ref if kind == "a" else vout_ref
            src = ref if h is None else ref.at[pl.ds(h * half, half)]
        plan.send((kind, ty, tx, h), src, slot(kind, ty, tx, h), device)

    def multiply(g, k):
        tok, val = ((tok_a, val_a), (tok_b, val_b))[k]
        for c in range(2):
            gram = lax.dot_general(
                tok[pl.ds(c * rows, rows), :], val[g], (((1,), (1,)), ((), ())), preferred_element_type=jnp.float32
            )
            part[g, k, :, pl.ds(c * block, block), :] = gram.reshape(NZ, block, NX * share)

    def add_up(g, k, n, t):
        sign, steps, base = ARCS[k][n]
        owner = (z + NZ + sign * (steps - t)) % NZ
        src = part.at[g, k, owner]
        stride = 2 if g == LAST else 1
        if t >= stride:
            src = hop.at[g, base + t - stride]
            src[...] = src[...] + part[g, k, owner]
        to = {"tensor": (z + NZ + sign * min(stride, steps - t)) % NZ}
        if g == LAST and k and t >= steps - stride:
            to["section"] = 1 - sec
        plan.send(("ring", g, k, n, t), src, hop.at[g, base + t], to)

    def reduced(g, k):
        total = part[g, k, z]
        for _, steps, base in ARCS[k]:
            total = total + hop[g, base + steps - 1]
            if g == LAST:
                total = total + hop[g, base + steps - 2]
        return total

    first = True
    for needs, (what, *at_) in ordered():
        for name in needs:
            if name == "local":
                for copy in local:
                    copy.wait()
            else:
                plan.arrived(name)
        if what == "go":
            go(*at_)
        elif what == "tok":
            plan.send("tok b", out_ref, tok_b.at[pl.ds(rows, rows)], sibling)
            plan.send("tok a", own_ref, tok_a.at[pl.ds(rows, rows)], sibling)
        elif what == "mul":
            multiply(*at_)
        elif what == "add":
            add_up(*at_)
        elif what == "keep":
            kept[at_[0]] = reduced(at_[0], 0)
        elif what == "give":
            plan.send(("cross", LAST), part.at[LAST, 1, z], got.at[LAST], partner)
        elif what == "cross":
            cross[at_[0]] = reduced(at_[0], 1)
            plan.send(("cross", at_[0]), cross.at[at_[0]], got.at[at_[0]], partner)
        elif what == "score":
            theirs = got[at_[0]]
            if at_[0] == LAST:
                for _, hops, base in ARCS[1]:
                    theirs = theirs + (hop[LAST, base + hops - 1] + hop[LAST, base + hops - 2])
            term = kept[at_[0]] * theirs
            total, first = (term if first else total + term), False

    scores = jnp.sum(total.T, axis=0, keepdims=True)
    tile[...] = jnp.zeros_like(tile)
    tile[0:1, 0:block] = scores[:, 0:block]
    tile[1:2, 0:block] = scores[:, block:]
    near = ({}, partner, sibling, diagonal)
    tiles[4 * z] = tile[...]
    for r in (4, 3, 5, 2, 6, 1, 7, 0):
        for j in range(4):
            if r or j:
                plan.send(("end", r, j), tile, tiles.at[4 * z + j], {**near[j], "tensor": (z + r) % NZ})
    plan.arrived(("end", 1, 0))
    tokens_ref[...] = (
        (tiles[4 * z, 0:1] + tiles[4 * z + 1, 0:1]) + (tiles[4 * z + 2, 1:2] + tiles[4 * z + 3, 1:2])
    )[:, 0:block]
    every = jnp.zeros_like(tiles[0, 0:1])
    for r in range(NZ):
        every = every + (
            (tiles[4 * r, 0:1] + tiles[4 * r + 1, 0:1]) + (tiles[4 * r + 2, 1:2] + tiles[4 * r + 3, 1:2])
        )
    seq_ref[...] = jnp.sum(every, axis=1, keepdims=True)
    plan.drain()
    assert len(plan.sems) == ARRIVALS


ARRIVALS = 84


def body(own_rows, out_rows, val_own, val_out):
    rows, wide_a = own_rows.shape[1:]
    share, wide_b = val_out.shape[1:]
    block, group = rows // NZ, NX * share
    f32, bf16 = jnp.float32, jnp.bfloat16
    hbm = pl.BlockSpec(memory_space=pl.ANY)
    vmem = pl.BlockSpec(memory_space=pltpu.VMEM)
    tokens, seq = pl.pallas_call(
        kernel,
        out_shape=(pltpu.VMEM((1, block), f32), pltpu.VMEM((1, 1), f32)),
        in_specs=[hbm] * 4,
        out_specs=(vmem, vmem),
        scratch_shapes=[
            pltpu.VMEM((2 * rows, wide_a), bf16),
            pltpu.VMEM((2 * rows, wide_b), bf16),
            pltpu.VMEM((NY, group, wide_a), bf16),
            pltpu.VMEM((NY, group, wide_b), bf16),
            pltpu.VMEM((NY, 2, NZ, 2 * block, group), f32),
            pltpu.VMEM((NY, 14, 2 * block, group), f32),
            pltpu.VMEM((NY, 2 * block, group), f32),
            pltpu.VMEM((NY, 2 * block, group), f32),
            pltpu.VMEM((NY, 2 * block, group), f32),
            pltpu.VMEM((8, 128), f32),
            pltpu.VMEM((4 * NZ, 8, 128), f32),
            pltpu.SemaphoreType.DMA((4,)),
            pltpu.SemaphoreType.DMA((7,)),
            pltpu.SemaphoreType.DMA((ARRIVALS,)),
        ],
        compiler_params=pltpu.CompilerParams(
            collective_id=0, has_side_effects=True, vmem_limit_bytes=62 * 1024 * 1024
        ),
    )(own_rows[0], out_rows[0], val_own[0], val_out[0])
    return tokens.reshape(block), seq.reshape(1)


def solution(mesh):
    spec = P("section", "dp", "tensor")
    return jax.shard_map(
        body,
        mesh=mesh,
        in_specs=(spec,) * 4,
        out_specs=(P(("dp", "tensor")), P("dp")),
        check_vma=False,
    )
```

```python
import jax
import jax.numpy as jnp
from jax import lax
from jax.experimental import pallas as pl
from jax.experimental.pallas import tpu as pltpu
from jax.sharding import PartitionSpec as P

NX = 4
NY = 4
NZ = 8
MESH = pl.DeviceIdType.MESH


ARCS = (((-1, 4, 0), (1, 3, 4)), ((1, 4, 7), (-1, 3, 11)))
HOLDS = {("a", "x"): 0.7, ("a", "y"): 1.41, ("b", "x"): 2.47, ("b", "y"): 4.93}
SUM_HOLDS = 0.7
LATENCY = {"x": 2.0, "y": 3.0, "z": 2.4, "c": 2.4}
SLACK = {0: 1.0, 3: 0.5, 1: 0.0, 2: 0.0}
AHEAD = 1.5
ISSUE, MULTIPLY = 0.08, (0.4, 1.0)
RANK = {0: 0, 3: 1, 1: 1, 2: 0}
LAST = 2
LINKS = {
    "e": ("a00-", "b000", "b001", "a030", "b030", "b300", "b301", "b330", "b100", "b101", "b130", "b200", "b201", "b230"),
    "w": ("a00-", "b001", "b000", "a011", "b011", "b300", "b301", "b101", "b311", "b100", "b111", "b201", "b200", "b211"),
    "n": ("b000", "b001", "a00-", "b300", "a03-", "a01-", "a020", "a021", "a300", "a330", "a310", "a320"),
    "s": ("b001", "b000", "a00-", "b101", "a01-", "a03-", "a021", "a020", "a101", "a111", "a131", "a121"),
}


def moved(dy, dx, to):
    sy, sx = {"n": (-1, 0), "s": (1, 0), "e": (0, -1), "w": (0, 1)}[to]
    return (dy + sy) % NY, (dx + sx) % NX


def steps():
    found = []
    for to, names in LINKS.items():
        axis = "y" if to in "ns" else "x"
        for n, name in enumerate(names):
            kind, dy, dx = name[0], int(name[1]), int(name[2])
            h = None if name[3] == "-" else int(name[3])
            needs = () if dy == dx == 0 else ((kind, dy, dx, h),)
            if n:
                needs += (("queued", to, n - 1),)
            held = HOLDS[kind, axis] * (2 if h is None else 1)
            found.append((n, needs, axis + to, held, (kind, *moved(dy, dx, to), h), ("go", kind, dy, dx, h, to)))
    found.append((0, (), "", 0.0, "tok", ("tok",)))
    for g in range(NY):
        for k, kind in enumerate("ab"):
            needs = [step[4] for step in found if step[4][:2] == (kind, g)]
            needs += ["local", "tok " + kind]
            found.append((60 + RANK[g], tuple(needs), "", MULTIPLY[k], ("mul", g, k), ("mul", g, k)))
            for n, (sign, hops, _) in enumerate(ARCS[k]):
                for t in range(hops):
                    stride = 2 if g == LAST else 1
                    needs = (("mul", g, k),) + ((("ring", g, k, n, t - stride),) if t >= stride else ())
                    if g == LAST:
                        needs += (("keep", 0), ("cross", 0))
                    sent = ("ring", g, k, n, t)
                    found.append((40 + RANK[g] - t / 8, needs, "z+" if sign > 0 else "z-", SUM_HOLDS, sent, ("add", g, k, n, t)))
            needs = tuple(("ring", g, k, n, hops - 1) for n, (_, hops, _) in enumerate(ARCS[k]))
            if g == LAST:
                needs += tuple(("ring", g, k, n, hops - 2) for n, (_, hops, _) in enumerate(ARCS[k]))
            if k and g == LAST:
                found.append((40, (("mul", g, k),), "c", SUM_HOLDS, ("cross", g), ("give",)))
                last = needs
            elif k:
                found.append((50 + RANK[g], needs, "c", SUM_HOLDS, ("cross", g), ("cross", g)))
            else:
                found.append((51 + RANK[g], needs, "", 0.1, ("keep", g), ("keep", g)))
        needs = (("cross", g), ("keep", g)) + (last if g == LAST else ())
        found.append((55 + RANK[g], needs, "", 0.1, ("score", g), ("score", g)))
    names = {step[4] for step in found} | {"local", "tok a", "tok b"}
    whole = lambda name: name if name in names or name[0] == "queued" else (*name[:3], None)
    return [(order, tuple(map(whole, needs)), *rest) for order, needs, *rest in found]


def ordered():
    left, arrives, free, now, seen, order = steps(), {"local": 4.0}, {}, 0.0, set(), []
    here = ("mul", "keep", "score", "queued")
    while left:
        best = None
        for step in left:
            if all(name in arrives for name in step[1]):
                ready = max([now] + [arrives[name] for name in step[1]])
                if step[2][:1] == "y":
                    ready = max(ready, free.get(step[2], 0.0) - AHEAD)
                if best is None or (ready, step[0]) < best[0]:
                    best = ((ready, step[0]), step)
        (ready, n), step = best
        left.remove(step)
        _, needs, link, held, sent, what = step
        order.append((tuple(name for name in needs if name not in seen and name[0] not in here), what))
        seen.update(needs)
        if link:
            now = ready + ISSUE
            free[link] = max(now, free.get(link, 0.0)) + held
            arrives[sent] = free[link] + LATENCY[link[0]] + (SLACK[sent[1]] if sent[0] == "ring" else 0.0)
            if what[0] == "go":
                arrives["queued", link[1], n] = now
        elif sent == "tok":
            now = ready + ISSUE
            arrives["tok b"], arrives["tok a"] = now + 6.0, now + 8.0
        else:
            now = arrives[sent] = ready + held
        TIMES.append((now, what))
    return order


TIMES = []


def together(name):
    what, *at_ = name if isinstance(name, tuple) else (name,)
    if what == "b" and (at_[1] == 2 or (at_[1], at_[2]) in ((NX - 1, 1), (1, 0))):
        return ("row b", at_[0])
    if what == "a" and at_[0] == 2:
        return ("row a",)
    if what == "ring" and at_[3] >= ARCS[at_[1]][at_[2]][1] - (2 if at_[0] == LAST else 1):
        return ("last sum" if at_[0] == LAST else "sum", at_[0], at_[1])
    if what == "end":
        return ("end",)
    return name


class Plan:
    def __init__(self, send_sem, recv_sem, sent, landed):
        self.send_sem, self.recv_sem, self.sent, self.landed = send_sem, recv_sem, sent, landed
        self.copies, self.sems, self.waited = {}, {}, set()

    def send(self, name, src, dst, device):
        what = name[0] if isinstance(name, tuple) else name
        n = self.sems.setdefault(together(name), len(self.sems))
        assert n < ARRIVALS
        copy = pltpu.make_async_remote_copy(
            src_ref=src,
            dst_ref=dst,
            send_sem=self.send_sem.at[list(self.sent).index(what)],
            recv_sem=self.recv_sem.at[n],
            device_id=device,
            device_id_type=MESH,
        )
        copy.start()
        self.copies[name] = copy

    def bytes_of(self, ref, send, recv):
        return pltpu.make_async_remote_copy(
            src_ref=ref,
            dst_ref=ref,
            send_sem=self.send_sem.at[send],
            recv_sem=self.recv_sem.at[recv],
            device_id={"tensor": lax.axis_index("tensor")},
            device_id_type=MESH,
        )

    def arrived(self, name):
        key = together(name)
        if key in self.waited:
            return
        self.waited.add(key)
        if key == name:
            self.copies[name].wait_recv()
        else:
            self.bytes_of(self.landed[key[0]], 0, self.sems[key]).wait_recv()

    def drain(self):
        for n, ref in enumerate(self.sent.values()):
            self.bytes_of(ref, n, 0).wait_send()


def kernel(
    own_ref, out_ref, vown_ref, vout_ref,
    tokens_ref, seq_ref,
    tok_a, tok_b, val_a, val_b, part, hop, kept, cross, got, tile, tiles,
    local_sem, send_sem, recv_sem,
):
    d, sec, z = lax.axis_index("dp"), lax.axis_index("section"), lax.axis_index("tensor")
    core, x, y = d % 2, (d // 2) % NX, d // (2 * NX)
    rows, share = own_ref.shape[0], vown_ref.shape[0]
    half, block = share // 2, rows // NZ

    def at(yy, xx, cc):
        return {"dp": (yy * NX + xx) * 2 + cc}

    east, west = at(y, (x + 1) % NX, core), at(y, (x + NX - 1) % NX, core)
    north, south = at((y + 1) % NY, x, core), at((y + NY - 1) % NY, x, core)
    sibling = at(y, x, 1 - core)
    partner = {"section": 1 - sec}
    diagonal = {"dp": sibling["dp"], "section": 1 - sec}
    up, down = {"tensor": (z + 1) % NZ}, {"tensor": (z + NZ - 1) % NZ}

    barrier = pltpu.get_barrier_semaphore()
    greeted = (east, west, north, south, sibling, partner, diagonal, up, down)
    for device in greeted:
        pl.semaphore_signal(barrier, inc=1, device_id=device, device_id_type=MESH)

    local = [
        pltpu.make_async_copy(vout_ref, val_b.at[0, pl.ds(0, share)], local_sem.at[0]),
        pltpu.make_async_copy(vown_ref, val_a.at[0, pl.ds(0, share)], local_sem.at[1]),
        pltpu.make_async_copy(out_ref, tok_b.at[pl.ds(0, rows)], local_sem.at[2]),
        pltpu.make_async_copy(own_ref, tok_a.at[pl.ds(0, rows)], local_sem.at[3]),
    ]
    for copy in local:
        copy.start()
    pl.semaphore_wait(barrier, len(greeted))

    count = {}
    for to in LINKS:
        for name in LINKS[to]:
            count[name[0]] = count.get(name[0], 0) + (share if name[3] == "-" else half)
    sent = {
        "a": tok_a.at[pl.ds(0, count["a"])],
        "b": tok_b.at[pl.ds(0, count["b"])],
        "tok a": own_ref,
        "tok b": out_ref,
        "ring": hop,
        "cross": cross,
        "end": tiles.at[pl.ds(0, 4 * NZ - 1)],
    }
    landed = {
        "row a": val_a.at[0],
        "row b": val_b.at[0, pl.ds(0, 4 * half)],
        "sum": hop.at[0, pl.ds(0, 2)],
        "last sum": hop.at[0, pl.ds(0, 4)],
        "end": tiles.at[pl.ds(0, 4 * NZ - 1)],
    }
    plan = Plan(send_sem, recv_sem, sent, landed)

    def slot(kind, dy, dx, h=None):
        ref = val_a if kind == "a" else val_b
        first, count = (dx * share, share) if h is None else (dx * share + h * half, half)
        return ref.at[dy, pl.ds(first, count)]

    def go(kind, dy, dx, h, to):
        device = {"n": north, "s": south, "e": east, "w": west}[to]
        ty, tx = moved(dy, dx, to)
        src = slot(kind, dy, dx, h)
        if dy == dx == 0:
            ref = vown_ref if kind == "a" else vout_ref
            src = ref if h is None else ref.at[pl.ds(h * half, half)]
        plan.send((kind, ty, tx, h), src, slot(kind, ty, tx, h), device)

    def multiply(g, k):
        tok, val = ((tok_a, val_a), (tok_b, val_b))[k]
        for c in range(2):
            gram = lax.dot_general(
                tok[pl.ds(c * rows, rows), :], val[g], (((1,), (1,)), ((), ())), preferred_element_type=jnp.float32
            )
            part[g, k, :, pl.ds(c * block, block), :] = gram.reshape(NZ, block, NX * share)

    def add_up(g, k, n, t):
        sign, steps, base = ARCS[k][n]
        owner = (z + NZ + sign * (steps - t)) % NZ
        src = part.at[g, k, owner]
        stride = 2 if g == LAST else 1
        if t >= stride:
            src = hop.at[g, base + t - stride]
            src[...] = src[...] + part[g, k, owner]
        to = {"tensor": (z + NZ + sign * min(stride, steps - t)) % NZ}
        if g == LAST and k and t >= steps - stride:
            to["section"] = 1 - sec
        plan.send(("ring", g, k, n, t), src, hop.at[g, base + t], to)

    def reduced(g, k):
        total = part[g, k, z]
        for _, steps, base in ARCS[k]:
            total = total + hop[g, base + steps - 1]
            if g == LAST:
                total = total + hop[g, base + steps - 2]
        return total

    first = True
    for needs, (what, *at_) in ordered():
        for name in needs:
            if name == "local":
                for copy in local:
                    copy.wait()
            else:
                plan.arrived(name)
        if what == "go":
            go(*at_)
        elif what == "tok":
            plan.send("tok b", out_ref, tok_b.at[pl.ds(rows, rows)], sibling)
            plan.send("tok a", own_ref, tok_a.at[pl.ds(rows, rows)], sibling)
        elif what == "mul":
            multiply(*at_)
        elif what == "add":
            add_up(*at_)
        elif what == "keep":
            kept[at_[0]] = reduced(at_[0], 0)
        elif what == "give":
            plan.send(("cross", LAST), part.at[LAST, 1, z], got.at[LAST], partner)
        elif what == "cross":
            cross[at_[0]] = reduced(at_[0], 1)
            plan.send(("cross", at_[0]), cross.at[at_[0]], got.at[at_[0]], partner)
        elif what == "score":
            theirs = got[at_[0]]
            if at_[0] == LAST:
                for _, hops, base in ARCS[1]:
                    theirs = theirs + (hop[LAST, base + hops - 1] + hop[LAST, base + hops - 2])
            term = kept[at_[0]] * theirs
            total, first = (term if first else total + term), False

    scores = jnp.sum(total.T, axis=0, keepdims=True)
    tile[...] = jnp.zeros_like(tile)
    tile[0:1, 0:block] = scores[:, 0:block]
    tile[1:2, 0:block] = scores[:, block:]
    near = ({}, partner, sibling, diagonal)
    tiles[4 * z] = tile[...]
    for r in (4, 3, 5, 2, 6, 1, 7, 0):
        for j in range(4):
            if r or j:
                plan.send(("end", r, j), tile, tiles.at[4 * z + j], {**near[j], "tensor": (z + r) % NZ})
    plan.arrived(("end", 1, 0))
    tokens_ref[...] = (
        (tiles[4 * z, 0:1] + tiles[4 * z + 1, 0:1]) + (tiles[4 * z + 2, 1:2] + tiles[4 * z + 3, 1:2])
    )[:, 0:block]
    every = jnp.zeros_like(tiles[0, 0:1])
    for r in range(NZ):
        every = every + (
            (tiles[4 * r, 0:1] + tiles[4 * r + 1, 0:1]) + (tiles[4 * r + 2, 1:2] + tiles[4 * r + 3, 1:2])
        )
    seq_ref[...] = jnp.sum(every, axis=1, keepdims=True)
    plan.drain()
    assert len(plan.sems) == ARRIVALS


ARRIVALS = 84


def body(own_rows, out_rows, val_own, val_out):
    rows, wide_a = own_rows.shape[1:]
    share, wide_b = val_out.shape[1:]
    block, group = rows // NZ, NX * share
    f32, bf16 = jnp.float32, jnp.bfloat16
    hbm = pl.BlockSpec(memory_space=pl.ANY)
    vmem = pl.BlockSpec(memory_space=pltpu.VMEM)
    tokens, seq = pl.pallas_call(
        kernel,
        out_shape=(pltpu.VMEM((1, block), f32), pltpu.VMEM((1, 1), f32)),
        in_specs=[hbm] * 4,
        out_specs=(vmem, vmem),
        scratch_shapes=[
            pltpu.VMEM((2 * rows, wide_a), bf16),
            pltpu.VMEM((2 * rows, wide_b), bf16),
            pltpu.VMEM((NY, group, wide_a), bf16),
            pltpu.VMEM((NY, group, wide_b), bf16),
            pltpu.VMEM((NY, 2, NZ, 2 * block, group), f32),
            pltpu.VMEM((NY, 14, 2 * block, group), f32),
            pltpu.VMEM((NY, 2 * block, group), f32),
            pltpu.VMEM((NY, 2 * block, group), f32),
            pltpu.VMEM((NY, 2 * block, group), f32),
            pltpu.VMEM((8, 128), f32),
            pltpu.VMEM((4 * NZ, 8, 128), f32),
            pltpu.SemaphoreType.DMA((4,)),
            pltpu.SemaphoreType.DMA((7,)),
            pltpu.SemaphoreType.DMA((ARRIVALS,)),
        ],
        compiler_params=pltpu.CompilerParams(
            collective_id=0, has_side_effects=True, vmem_limit_bytes=62 * 1024 * 1024
        ),
    )(own_rows[0], out_rows[0], val_own[0], val_out[0])
    return tokens.reshape(block), seq.reshape(1)


def solution(mesh):
    spec = P("section", "dp", "tensor")
    return jax.shard_map(
        body,
        mesh=mesh,
        in_specs=(spec,) * 4,
        out_specs=(P(("dp", "tensor")), P("dp")),
        check_vma=False,
    )
```

```python
import jax
import jax.numpy as jnp
from jax import lax
from jax.experimental import pallas as pl
from jax.experimental.pallas import tpu as pltpu
from jax.sharding import PartitionSpec as P

NX = 4
NY = 4
NZ = 8
MESH = pl.DeviceIdType.MESH


ARCS = (((-1, 4, 0), (1, 3, 4)), ((1, 4, 7), (-1, 3, 11)))
HOLDS = {("a", "x"): 0.7, ("a", "y"): 1.41, ("b", "x"): 2.47, ("b", "y"): 4.93}
SUM_HOLDS = 0.7
LATENCY = {"x": 2.0, "y": 3.0, "z": 2.4, "c": 2.4}
SLACK = {0: 1.0, 3: 0.5, 1: 0.0, 2: 0.0}
AHEAD = 1.5
ISSUE, MULTIPLY = 0.08, (0.45, 1.15)
RANK = {0: 0, 3: 1, 1: 1, 2: 0}
LAST = 2
LINKS = {
    "e": ("a00-", "b000", "b001", "a030", "b030", "b300", "b301", "b330", "b100", "b101", "b130", "b200", "b201", "b230"),
    "w": ("a00-", "b001", "b000", "a011", "b011", "b300", "b301", "b101", "b311", "b100", "b111", "b201", "b200", "b211"),
    "n": ("b000", "b001", "a00-", "b300", "a03-", "a01-", "a020", "a021", "a300", "a330", "a310", "a320"),
    "s": ("b001", "b000", "a00-", "b101", "a01-", "a03-", "a021", "a020", "a101", "a111", "a131", "a121"),
}


def moved(dy, dx, to):
    sy, sx = {"n": (-1, 0), "s": (1, 0), "e": (0, -1), "w": (0, 1)}[to]
    return (dy + sy) % NY, (dx + sx) % NX


def steps():
    found = []
    for to, names in LINKS.items():
        axis = "y" if to in "ns" else "x"
        for n, name in enumerate(names):
            kind, dy, dx = name[0], int(name[1]), int(name[2])
            h = None if name[3] == "-" else int(name[3])
            needs = () if dy == dx == 0 else ((kind, dy, dx, h),)
            if n:
                needs += (("queued", to, n - 1),)
            held = HOLDS[kind, axis] * (2 if h is None else 1)
            found.append((n, needs, axis + to, held, (kind, *moved(dy, dx, to), h), ("go", kind, dy, dx, h, to)))
    found.append((0, (), "", 0.0, "tok", ("tok",)))
    for g in range(NY):
        for k, kind in enumerate("ab"):
            needs = [step[4] for step in found if step[4][:2] == (kind, g)]
            needs += ["local", "tok " + kind]
            found.append((60 + RANK[g], tuple(needs), "", MULTIPLY[k], ("mul", g, k), ("mul", g, k)))
            for n, (sign, hops, _) in enumerate(ARCS[k]):
                for t in range(hops):
                    stride = 2 if g == LAST else 1
                    needs = (("mul", g, k),) + ((("ring", g, k, n, t - stride),) if t >= stride else ())
                    if g == LAST:
                        needs += (("keep", 0), ("cross", 0))
                    sent = ("ring", g, k, n, t)
                    found.append((40 + RANK[g] - t / 8, needs, "z+" if sign > 0 else "z-", SUM_HOLDS, sent, ("add", g, k, n, t)))
            needs = tuple(("ring", g, k, n, hops - 1) for n, (_, hops, _) in enumerate(ARCS[k]))
            if g == LAST:
                needs += tuple(("ring", g, k, n, hops - 2) for n, (_, hops, _) in enumerate(ARCS[k]))
            if k and g == LAST:
                found.append((40, (("mul", g, k),), "c", SUM_HOLDS, ("cross", g), ("give",)))
                last = needs
            elif k:
                found.append((50 + RANK[g], needs, "c", SUM_HOLDS, ("cross", g), ("cross", g)))
            else:
                found.append((51 + RANK[g], needs, "", 0.1, ("keep", g), ("keep", g)))
        needs = (("cross", g), ("keep", g)) + (last if g == LAST else ())
        found.append((55 + RANK[g], needs, "", 0.1, ("score", g), ("score", g)))
    names = {step[4] for step in found} | {"local", "tok a", "tok b"}
    whole = lambda name: name if name in names or name[0] == "queued" else (*name[:3], None)
    return [(order, tuple(map(whole, needs)), *rest) for order, needs, *rest in found]


def ordered():
    left, arrives, free, now, seen, order = steps(), {"local": 4.0}, {}, 0.0, set(), []
    here = ("mul", "keep", "score", "queued")
    while left:
        best = None
        for step in left:
            if all(name in arrives for name in step[1]):
                ready = max([now] + [arrives[name] for name in step[1]])
                if step[2][:1] == "y":
                    ready = max(ready, free.get(step[2], 0.0) - AHEAD)
                if best is None or (ready, step[0]) < best[0]:
                    best = ((ready, step[0]), step)
        (ready, n), step = best
        left.remove(step)
        _, needs, link, held, sent, what = step
        order.append((tuple(name for name in needs if name not in seen and name[0] not in here), what))
        seen.update(needs)
        if link:
            now = ready + ISSUE
            free[link] = max(now, free.get(link, 0.0)) + held
            arrives[sent] = free[link] + LATENCY[link[0]] + (SLACK[sent[1]] if sent[0] == "ring" else 0.0)
            if what[0] == "go":
                arrives["queued", link[1], n] = now
        elif sent == "tok":
            now = ready + ISSUE
            arrives["tok b"], arrives["tok a"] = now + 6.0, now + 8.0
        else:
            now = arrives[sent] = ready + held
        TIMES.append((now, what))
    return order


TIMES = []


def together(name):
    what, *at_ = name if isinstance(name, tuple) else (name,)
    if what == "b" and (at_[1] == 2 or (at_[1], at_[2]) in ((NX - 1, 1), (1, 0))):
        return ("row b", at_[0])
    if what == "a" and at_[0] == 2:
        return ("row a",)
    if what == "ring" and at_[3] >= ARCS[at_[1]][at_[2]][1] - (2 if at_[0] == LAST else 1):
        return ("last sum" if at_[0] == LAST else "sum", at_[0], at_[1])
    if what == "end":
        return ("end",)
    return name


class Plan:
    def __init__(self, send_sem, recv_sem, sent, landed):
        self.send_sem, self.recv_sem, self.sent, self.landed = send_sem, recv_sem, sent, landed
        self.copies, self.sems, self.waited = {}, {}, set()

    def send(self, name, src, dst, device):
        what = name[0] if isinstance(name, tuple) else name
        n = self.sems.setdefault(together(name), len(self.sems))
        assert n < ARRIVALS
        copy = pltpu.make_async_remote_copy(
            src_ref=src,
            dst_ref=dst,
            send_sem=self.send_sem.at[list(self.sent).index(what)],
            recv_sem=self.recv_sem.at[n],
            device_id=device,
            device_id_type=MESH,
        )
        copy.start()
        self.copies[name] = copy

    def bytes_of(self, ref, send, recv):
        return pltpu.make_async_remote_copy(
            src_ref=ref,
            dst_ref=ref,
            send_sem=self.send_sem.at[send],
            recv_sem=self.recv_sem.at[recv],
            device_id={"tensor": lax.axis_index("tensor")},
            device_id_type=MESH,
        )

    def arrived(self, name):
        key = together(name)
        if key in self.waited:
            return
        self.waited.add(key)
        if key == name:
            self.copies[name].wait_recv()
        else:
            self.bytes_of(self.landed[key[0]], 0, self.sems[key]).wait_recv()

    def drain(self):
        for n, ref in enumerate(self.sent.values()):
            self.bytes_of(ref, n, 0).wait_send()


def kernel(
    own_ref, out_ref, vown_ref, vout_ref,
    tokens_ref, seq_ref,
    tok_a, tok_b, val_a, val_b, part, hop, kept, cross, got, tile, tiles,
    local_sem, send_sem, recv_sem,
):
    d, sec, z = lax.axis_index("dp"), lax.axis_index("section"), lax.axis_index("tensor")
    core, x, y = d % 2, (d // 2) % NX, d // (2 * NX)
    rows, share = own_ref.shape[0], vown_ref.shape[0]
    half, block = share // 2, rows // NZ

    def at(yy, xx, cc):
        return {"dp": (yy * NX + xx) * 2 + cc}

    east, west = at(y, (x + 1) % NX, core), at(y, (x + NX - 1) % NX, core)
    north, south = at((y + 1) % NY, x, core), at((y + NY - 1) % NY, x, core)
    sibling = at(y, x, 1 - core)
    partner = {"section": 1 - sec}
    diagonal = {"dp": sibling["dp"], "section": 1 - sec}
    up, down = {"tensor": (z + 1) % NZ}, {"tensor": (z + NZ - 1) % NZ}

    barrier = pltpu.get_barrier_semaphore()
    greeted = (east, west, north, south, sibling, partner, diagonal, up, down)
    for device in greeted:
        pl.semaphore_signal(barrier, inc=1, device_id=device, device_id_type=MESH)

    local = [
        pltpu.make_async_copy(vout_ref, val_b.at[0, pl.ds(0, share)], local_sem.at[0]),
        pltpu.make_async_copy(vown_ref, val_a.at[0, pl.ds(0, share)], local_sem.at[1]),
        pltpu.make_async_copy(out_ref, tok_b.at[pl.ds(0, rows)], local_sem.at[2]),
        pltpu.make_async_copy(own_ref, tok_a.at[pl.ds(0, rows)], local_sem.at[3]),
    ]
    for copy in local:
        copy.start()
    pl.semaphore_wait(barrier, len(greeted))

    count = {}
    for to in LINKS:
        for name in LINKS[to]:
            count[name[0]] = count.get(name[0], 0) + (share if name[3] == "-" else half)
    sent = {
        "a": tok_a.at[pl.ds(0, count["a"])],
        "b": tok_b.at[pl.ds(0, count["b"])],
        "tok a": own_ref,
        "tok b": out_ref,
        "ring": hop,
        "cross": cross,
        "end": tiles.at[pl.ds(0, 4 * NZ - 1)],
    }
    landed = {
        "row a": val_a.at[0],
        "row b": val_b.at[0, pl.ds(0, 4 * half)],
        "sum": hop.at[0, pl.ds(0, 2)],
        "last sum": hop.at[0, pl.ds(0, 4)],
        "end": tiles.at[pl.ds(0, 4 * NZ - 1)],
    }
    plan = Plan(send_sem, recv_sem, sent, landed)

    def slot(kind, dy, dx, h=None):
        ref = val_a if kind == "a" else val_b
        first, count = (dx * share, share) if h is None else (dx * share + h * half, half)
        return ref.at[dy, pl.ds(first, count)]

    def go(kind, dy, dx, h, to):
        device = {"n": north, "s": south, "e": east, "w": west}[to]
        ty, tx = moved(dy, dx, to)
        src = slot(kind, dy, dx, h)
        if dy == dx == 0:
            ref = vown_ref if kind == "a" else vout_ref
            src = ref if h is None else ref.at[pl.ds(h * half, half)]
        plan.send((kind, ty, tx, h), src, slot(kind, ty, tx, h), device)

    def multiply(g, k):
        tok, val = ((tok_a, val_a), (tok_b, val_b))[k]
        for c in range(2):
            gram = lax.dot_general(
                tok[pl.ds(c * rows, rows), :], val[g], (((1,), (1,)), ((), ())), preferred_element_type=jnp.float32
            )
            part[g, k, :, pl.ds(c * block, block), :] = gram.reshape(NZ, block, NX * share)

    def add_up(g, k, n, t):
        sign, steps, base = ARCS[k][n]
        owner = (z + NZ + sign * (steps - t)) % NZ
        src = part.at[g, k, owner]
        stride = 2 if g == LAST else 1
        if t >= stride:
            src = hop.at[g, base + t - stride]
            src[...] = src[...] + part[g, k, owner]
        to = {"tensor": (z + NZ + sign * min(stride, steps - t)) % NZ}
        if g == LAST and k and t >= steps - stride:
            to["section"] = 1 - sec
        plan.send(("ring", g, k, n, t), src, hop.at[g, base + t], to)

    def reduced(g, k):
        total = part[g, k, z]
        for _, steps, base in ARCS[k]:
            total = total + hop[g, base + steps - 1]
            if g == LAST:
                total = total + hop[g, base + steps - 2]
        return total

    first = True
    for needs, (what, *at_) in ordered():
        for name in needs:
            if name == "local":
                for copy in local:
                    copy.wait()
            else:
                plan.arrived(name)
        if what == "go":
            go(*at_)
        elif what == "tok":
            plan.send("tok b", out_ref, tok_b.at[pl.ds(rows, rows)], sibling)
            plan.send("tok a", own_ref, tok_a.at[pl.ds(rows, rows)], sibling)
        elif what == "mul":
            multiply(*at_)
        elif what == "add":
            add_up(*at_)
        elif what == "keep":
            kept[at_[0]] = reduced(at_[0], 0)
        elif what == "give":
            plan.send(("cross", LAST), part.at[LAST, 1, z], got.at[LAST], partner)
        elif what == "cross":
            cross[at_[0]] = reduced(at_[0], 1)
            plan.send(("cross", at_[0]), cross.at[at_[0]], got.at[at_[0]], partner)
        elif what == "score":
            theirs = got[at_[0]]
            if at_[0] == LAST:
                for _, hops, base in ARCS[1]:
                    theirs = theirs + (hop[LAST, base + hops - 1] + hop[LAST, base + hops - 2])
            term = kept[at_[0]] * theirs
            total, first = (term if first else total + term), False

    scores = jnp.sum(total.T, axis=0, keepdims=True)
    tile[...] = jnp.zeros_like(tile)
    tile[0:1, 0:block] = scores[:, 0:block]
    tile[1:2, 0:block] = scores[:, block:]
    near = ({}, partner, sibling, diagonal)
    tiles[4 * z] = tile[...]
    for r in (4, 3, 5, 2, 6, 1, 7, 0):
        for j in range(4):
            if r or j:
                plan.send(("end", r, j), tile, tiles.at[4 * z + j], {**near[j], "tensor": (z + r) % NZ})
    plan.arrived(("end", 1, 0))
    tokens_ref[...] = (
        (tiles[4 * z, 0:1] + tiles[4 * z + 1, 0:1]) + (tiles[4 * z + 2, 1:2] + tiles[4 * z + 3, 1:2])
    )[:, 0:block]
    every = jnp.zeros_like(tiles[0, 0:1])
    for r in range(NZ):
        every = every + (
            (tiles[4 * r, 0:1] + tiles[4 * r + 1, 0:1]) + (tiles[4 * r + 2, 1:2] + tiles[4 * r + 3, 1:2])
        )
    seq_ref[...] = jnp.sum(every, axis=1, keepdims=True)
    plan.drain()
    assert len(plan.sems) == ARRIVALS


ARRIVALS = 84


def body(own_rows, out_rows, val_own, val_out):
    rows, wide_a = own_rows.shape[1:]
    share, wide_b = val_out.shape[1:]
    block, group = rows // NZ, NX * share
    f32, bf16 = jnp.float32, jnp.bfloat16
    hbm = pl.BlockSpec(memory_space=pl.ANY)
    vmem = pl.BlockSpec(memory_space=pltpu.VMEM)
    tokens, seq = pl.pallas_call(
        kernel,
        out_shape=(pltpu.VMEM((1, block), f32), pltpu.VMEM((1, 1), f32)),
        in_specs=[hbm] * 4,
        out_specs=(vmem, vmem),
        scratch_shapes=[
            pltpu.VMEM((2 * rows, wide_a), bf16),
            pltpu.VMEM((2 * rows, wide_b), bf16),
            pltpu.VMEM((NY, group, wide_a), bf16),
            pltpu.VMEM((NY, group, wide_b), bf16),
            pltpu.VMEM((NY, 2, NZ, 2 * block, group), f32),
            pltpu.VMEM((NY, 14, 2 * block, group), f32),
            pltpu.VMEM((NY, 2 * block, group), f32),
            pltpu.VMEM((NY, 2 * block, group), f32),
            pltpu.VMEM((NY, 2 * block, group), f32),
            pltpu.VMEM((8, 128), f32),
            pltpu.VMEM((4 * NZ, 8, 128), f32),
            pltpu.SemaphoreType.DMA((4,)),
            pltpu.SemaphoreType.DMA((7,)),
            pltpu.SemaphoreType.DMA((ARRIVALS,)),
        ],
        compiler_params=pltpu.CompilerParams(
            collective_id=0, has_side_effects=True, vmem_limit_bytes=62 * 1024 * 1024
        ),
    )(own_rows[0], out_rows[0], val_own[0], val_out[0])
    return tokens.reshape(block), seq.reshape(1)


def solution(mesh):
    spec = P("section", "dp", "tensor")
    return jax.shard_map(
        body,
        mesh=mesh,
        in_specs=(spec,) * 4,
        out_specs=(P(("dp", "tensor")), P("dp")),
        check_vma=False,
    )
```
